256 devices in a mesh: dp: 128 (over x, z, y), rep: 2 (over core).
Axes of the slice: x: 4, y: 4, z: 8, core: 2. Of those that a mesh axis runs over, the one named last changes fastest.
Arguments:
- features: bfloat16 [32768, 1024], P(('dp', 'rep')), may hold values from -6 to 6
- cotangent: bfloat16 [32768, 1024], P(('dp', 'rep')), may hold values from -6 to 6
- routes: int32 [32768, 2], P(('dp', 'rep')), may hold values from 0 to 127, all different within a row; in each aligned block of 128 rows (0 to 127, 128 to 255, ...) at most 3 rows name the same one
- route_weights: float32 [32768, 2], P(('dp', 'rep')), may hold values from 0.2 to 1
- counts: int32 [32768], P(('dp', 'rep')), may hold values from 1 to 4
- cross_weight: bfloat16 [1024, 1024], P(('dp', 'rep')), may hold values from -0.1875 to 0.1875
- gate_weight: bfloat16 [1024, 1024], P(('dp', 'rep')), may hold values from -0.1875 to 0.1875
- cross_bias: float32 [1024], replicated, may hold values from -3 to 3
- gate_bias: float32 [1024], replicated, may hold values from -4 to 4
- expert_in: bfloat16 [128, 1024, 2048], P('dp', None, 'rep'), may hold values from -0.1875 to 0.1875
- expert_out: bfloat16 [128, 2048, 1024], P('dp', 'rep'), may hold values from -0.125 to 0.125
Outputs:
- layer_output: bfloat16 [32768, 1024], P(('dp', 'rep'))
- grad_cross_weight: bfloat16 [1024, 1024], P('rep')
- grad_gate_weight: bfloat16 [1024, 1024], P('rep')
- grad_cross_bias: float32 [1024], P('rep')
- grad_gate_bias: float32 [1024], P('rep')
- grad_expert_in: bfloat16 [128, 1024, 2048], P('dp', None, 'rep')
- grad_expert_out: bfloat16 [128, 2048, 1024], P('dp', 'rep')
The draws below stay inside these ranges and needn't reach their ends.
Inputs may be any that keep to these rules, and one draw needn't show every extreme that they name: `routes`: the two experts of a row differ. In the rows of one device (aligned blocks of 128 rows) no expert is named more than 3 times, and in every draw some expert is named exactly 3 times in some block. Every expert is named by some row.
All inputs are finite; a program needn't handle non-finite values.
Results may differ from the reference program's by a relative error of at most 0.02.
Values may be sent and summed in bfloat16 or wider, within the bound.
No kernel may reach another device: no remote copies, remote signals or barrier semaphores. Data moves between devices by JAX's collectives and lax.ppermute only.
A program may use at most 128 MiB of HBM per device.

```python
import math
import jax
import jax.numpy as jnp
import numpy as np
from jax import lax

D = 1024
FF = 2048
TOK_DEV = 128
EXPERTS = 128
CAP = 3
TOKENS = 32768
N_DP = 128
N_REP = 2


def touch_ends(entries, stream_key, least, top_value):
    shape = entries.shape
    spot = [jax.random.randint(jax.random.fold_in(stream_key, axis), (), 0, shape[axis]) for axis in range(len(shape))]
    entries = entries.at[tuple(spot)].set(least)
    longest = shape.index(max(shape))
    spot[longest] = (spot[longest] + 1) % shape[longest]
    return entries.at[tuple(spot)].set(top_value)


def shard_levels(rng, dims, shards, least, top_value):
    factor_of, own = 1.0, jax.random.fold_in(rng, 6)
    for dim, blocks in shards:
        steps = jnp.exp(jax.random.uniform(jax.random.fold_in(own, dim), (blocks,), jnp.float32, least / len(shards), top_value / len(shards)))
        factor_of = factor_of * jnp.repeat(steps, dims[dim] // blocks).reshape([-1 if axis == dim else 1 for axis in range(len(dims))])
    return factor_of


def shared_out(rng, own, number, rows, amount, top, bound, skew):
    order = jax.random.permutation(rng, amount)
    crowded, ordinary = portions_of(amount, rows * top, bound, skew, True), portions_of(amount, rows * top, bound, skew, False)
    places = jnp.arange(amount)

    def named(sizes, offset_by):
        used = int((sizes > 0).sum())
        fixed = max(1, used // 4)
        moved = fixed + (places - fixed + offset_by * (used - fixed)) % max(1, amount - fixed)
        return jnp.zeros((amount,), jnp.int32).at[order[jnp.where(places < fixed, places, moved)]].set(jnp.asarray(sizes, jnp.int32))

    sizes = jnp.where(number % 4 == 0, named(crowded, number // 4), named(ordinary, number - number // 4 - 1))
    mixed = jax.random.permutation(jax.random.fold_in(own, 3), amount)
    giver, taker = mixed[0:amount // 2 * 2:2], mixed[1:amount // 2 * 2:2]
    slack = jnp.minimum(sizes[giver] - 1, bound - sizes[taker]) // 2
    slack = jnp.where((giver == order[0]) | (taker == order[0]) | (sizes[taker] == 0), 0, jnp.maximum(slack, 0))
    moved = jax.random.randint(jax.random.fold_in(own, 4), (amount // 2,), 0, 1 << 20) % (slack + 1)
    sizes = sizes.at[giver].add(-moved).at[taker].add(moved)
    labels = jnp.searchsorted(jnp.cumsum(sizes), jnp.arange(rows * top), side="right").astype(jnp.int32)
    table = labels.reshape(top, rows).T
    table = table[jax.random.permutation(jax.random.fold_in(own, 1), rows)]
    offset_by = jax.random.randint(jax.random.fold_in(own, 2), (rows, 1), 0, top)
    return jnp.take_along_axis(table, (jnp.arange(top)[None, :] + offset_by) % top, axis=1)


def portions_of(number_of, total, most, slope, full):
    weights = [(1 << 20) // math.isqrt(grade ** slope) + 1 for grade in range(1, number_of + 1)]
    largest = most if full else min(most, max(-(-total // number_of), total * weights[0] // sum(weights)))
    least = 1 if total - largest >= number_of - 1 else 0
    holding, rest = [largest] + [least] * (number_of - 1), total - largest - least * (number_of - 1)
    while rest > 0:
        candidates = [i for i in range(1, number_of) if holding[i] < largest] or [i for i in range(1, number_of) if holding[i] < most]
        pool, left = sum([weights[i] for i in candidates]), rest
        for i in candidates:
            addition = min(most - holding[i], max(1, left * weights[i] // pool), rest)
            holding[i] = holding[i] + addition
            rest = rest - addition
    return np.array(holding)


def noise(key, shape, scale, limit, split=(), kind=jnp.bfloat16):
    entries = jax.random.normal(key, shape, jnp.float32) * scale
    if len(split) > 0:
        entries = shard_levels(key, shape, split, -0.22, 0.18) * entries
    return jnp.clip(entries, min=-limit, max=limit).astype(kind)


def setup_inputs(seed: int = 0) -> dict:
    key_list = jax.random.split(jax.random.key(seed), 12)
    features = noise(key_list[0], (TOKENS, D), 1.0, 6.0, ((0, 256),))
    cotangent = noise(key_list[1], (TOKENS, D), 1.0, 6.0, ((0, 256),))
    routes_keys = jax.random.split(jax.random.fold_in(key_list[2], 1), TOKENS // TOK_DEV)
    routes_turns = jax.random.permutation(jax.random.fold_in(key_list[2], 3), TOKENS // TOK_DEV)
    routes = jax.vmap(lambda own, number: shared_out(jax.random.fold_in(key_list[2], 2), own, number, TOK_DEV, EXPERTS, 2, CAP, 2))(routes_keys, routes_turns).reshape((TOKENS, 2))
    route_weights = jnp.clip(0.2 + 0.8 * jax.random.uniform(key_list[3], (TOKENS, 2), jnp.float32) ** shard_levels(key_list[3], (TOKENS, 2), ((0, 256),), -0.2, 0.2), 0.2, 1.0)
    counts = touch_ends(jax.random.randint(key_list[4], (TOKENS,), 1, 5), jax.random.fold_in(key_list[4], 1), 1, 4).astype(jnp.int32)
    cross_weight = noise(key_list[5], (D, D), D ** -0.5, 0.1875, ((0, 256),))
    gate_weight = noise(key_list[6], (D, D), D ** -0.5, 0.1875, ((0, 256),))
    cross_bias = noise(key_list[7], (D,), 0.5, 3.0, (), jnp.float32)
    gate_bias = noise(key_list[8], (D,), 1.0, 4.0, (), jnp.float32)
    expert_in = noise(key_list[9], (EXPERTS, D, FF), D ** -0.5, 0.1875, ((0, 128), (2, 2)))
    expert_out = noise(key_list[10], (EXPERTS, FF, D), FF ** -0.5, 0.125, ((0, 128), (1, 2)))
    return {"features": features, "cotangent": cotangent, "routes": routes, "route_weights": route_weights, "counts": counts, "cross_weight": cross_weight, "gate_weight": gate_weight, "cross_bias": cross_bias, "gate_bias": gate_bias, "expert_in": expert_in, "expert_out": expert_out}


def reference(features, cotangent, routes, route_weights, counts, cross_weight, gate_weight, cross_bias, gate_bias, expert_in, expert_out):
    cross_term = jnp.dot(features, cross_weight, preferred_element_type=jnp.float32) + cross_bias
    gate_term = jax.nn.sigmoid(jnp.dot(features, gate_weight, preferred_element_type=jnp.float32) + gate_bias)
    feature_f = features.astype(jnp.float32)
    crossed = (feature_f * cross_term * gate_term + feature_f).astype(jnp.bfloat16)

    blocks = N_DP * N_REP
    width = D
    block_routes = routes.reshape(blocks, 2 * TOK_DEV)
    onehot = (block_routes[:, :, None] == jnp.arange(EXPERTS, dtype=jnp.int32)[None, None, :]).astype(jnp.int32)
    position = jnp.sum((jnp.cumsum(onehot, axis=1) - 1) * onehot, axis=2)
    slot_index = (jnp.arange(blocks, dtype=jnp.int32)[:, None] * CAP + position).reshape(-1).astype(jnp.int32)
    expert_of = routes.reshape(-1).astype(jnp.int32)
    slot_table = jnp.full((EXPERTS, blocks * CAP), -1, jnp.int32)
    slot_table = slot_table.at[expert_of, slot_index].set(jnp.arange(2 * TOKENS, dtype=jnp.int32))

    upstream = 0.05 * counts.astype(jnp.float32)[:, None] * cotangent.astype(jnp.float32)
    out_grad = (route_weights[:, :, None] * upstream[:, None, :]).astype(jnp.bfloat16).reshape(2 * TOKENS, width)

    def per_expert(packed):
        sources, weight_in, weight_out = packed
        filled = sources >= 0
        source = jnp.where(filled, sources, 0).astype(jnp.int32)
        slot_rows = jnp.where(filled[:, None], crossed[source // 2], jnp.zeros((), jnp.bfloat16))
        slot_grads = jnp.where(filled[:, None], out_grad[source], jnp.zeros((), jnp.bfloat16))
        pre_act = jnp.dot(slot_rows, weight_in, preferred_element_type=jnp.float32)
        squash = jax.nn.sigmoid(pre_act)
        hidden = (pre_act * squash).astype(jnp.bfloat16)
        result = jnp.dot(hidden, weight_out, preferred_element_type=jnp.float32).astype(jnp.bfloat16)
        hid_grad = jnp.dot(slot_grads, weight_out.T, preferred_element_type=jnp.float32)
        pre_grad = (hid_grad * squash * (1.0 + pre_act * (1.0 - squash))).astype(jnp.bfloat16)
        back_rows = jnp.dot(pre_grad, weight_in.T, preferred_element_type=jnp.float32).astype(jnp.bfloat16)
        grad_in = jnp.dot(slot_rows.T, pre_grad, preferred_element_type=jnp.float32).astype(jnp.bfloat16)
        grad_out = jnp.dot(hidden.T, slot_grads, preferred_element_type=jnp.float32).astype(jnp.bfloat16)
        return result, back_rows, grad_in, grad_out

    expert_outs, expert_backs, grad_expert_in, grad_expert_out = lax.map(per_expert, (slot_table, expert_in, expert_out))

    slot_flat = (expert_of * (blocks * CAP) + slot_index).astype(jnp.int32)
    out_rows = expert_outs.reshape(-1, width)[slot_flat].reshape(TOKENS, 2, width).astype(jnp.float32)
    layer_output = (crossed.astype(jnp.float32) + jnp.sum(route_weights[:, :, None] * out_rows, axis=1)).astype(jnp.bfloat16)
    back_gathered = expert_backs.reshape(-1, width)[slot_flat].reshape(TOKENS, 2, width).astype(jnp.float32)
    crossed_grad = upstream + jnp.sum(back_gathered, axis=1)
    cross_grad = (crossed_grad * feature_f * gate_term).astype(jnp.bfloat16)
    gate_grad = (crossed_grad * feature_f * cross_term * gate_term * (1.0 - gate_term)).astype(jnp.bfloat16)
    grad_cross_weight = jnp.dot(features.T, cross_grad, preferred_element_type=jnp.float32).astype(jnp.bfloat16)
    grad_gate_weight = jnp.dot(features.T, gate_grad, preferred_element_type=jnp.float32).astype(jnp.bfloat16)
    grad_cross_bias = jnp.sum(cross_grad.astype(jnp.float32), axis=0)
    grad_gate_bias = jnp.sum(gate_grad.astype(jnp.float32), axis=0)
    return (layer_output, grad_cross_weight, grad_gate_weight, grad_cross_bias, grad_gate_bias, grad_expert_in, grad_expert_out)
```

```python
import jax
import jax.numpy as jnp
from jax import lax
from jax.experimental import pallas as pl
from jax.experimental.pallas import tpu as pltpu
from jax.sharding import Mesh, PartitionSpec as P


NX, NZ, NY = 4, 8, 4
ALL = ("x", "z", "y", "rep")
DP = ("x", "z", "y")
PLANE = ("x", "y")
COLUMN = ("z", "rep")
CAP = 3
TAIL = 16
F32 = jnp.float32
BF16 = jnp.bfloat16


def swap(v):
    return lax.ppermute(v, "rep", [(0, 1), (1, 0)])


def exchange(v, axes):
    return lax.all_to_all(v, axes, split_axis=0, concat_axis=0, tiled=True)


def spread(v, axes, count):
    return exchange(jnp.broadcast_to(v[None], (count,) + v.shape), axes)


def ring(v, axis):
    return [v] + [
        lax.ppermute(v, axis, [(i, (i + k) % 4) for i in range(4)]) for k in range(1, 4)
    ]


def gather_plane(v, split):
    upper = jnp.concatenate(ring(v[:split], "y"), axis=0)
    lower = jnp.concatenate(ring(v[split:], "x"), axis=0)
    return ring(upper, "x") + ring(lower, "y")


def dot(a, b, dims=((1,), (0,))):
    return lax.dot_general(a, b, (dims, ((), ())), preferred_element_type=F32)


def dispatch(rows, experts_n):
    width = rows.shape[1]
    packed = rows.reshape(experts_n, CAP * width // 128, 128)
    got = exchange(packed, DP)
    return got.reshape(experts_n * CAP, width)


def project_kernel(rows, *refs):
    *parts, own, sent = refs
    total = jnp.zeros((256, 1024), F32)
    for k, part in enumerate(parts):
        total += jnp.dot(
            rows[:, 128 * k : 128 * k + 128], part[...], preferred_element_type=F32
        )
    own[...] = total[:128]
    sent[...] = total[128:]


def part_kernel(pos, *refs):
    *parts, block, out = refs
    x, y = pos[0], pos[1]
    total = jnp.zeros((128, 1024), F32)
    bias = jnp.zeros((1, 128), F32)
    for n, part in enumerate(parts):
        got = []
        for m in range(4):
            kx, ky = (n, m) if n < 4 else (m, n - 4)
            source = ((x - kx + 4) & 3) * 4 + ((y - ky + 4) & 3)
            rows = slice(0, 64) if n < 4 else slice(64, 128)
            got.append(block[source, rows, :])
        got = jnp.concatenate(got, axis=0)
        total += lax.dot_general(
            got, part[...], (((0,), (0,)), ((), ())), preferred_element_type=F32
        )
        bias += jnp.sum(got.astype(F32), axis=0, keepdims=True)
    part = total.T.astype(BF16)
    high = bias.astype(BF16).astype(F32)
    row = lax.broadcasted_iota(jnp.int32, (TAIL, 128), 0)
    tail = jnp.where(row == 0, high, jnp.where(row == 1, bias - high, 0.0)).astype(BF16)
    for z in range(NZ):
        for r in range(2):
            out[2 * z + r, :64, :] = part[r * 512 + z * 64 : r * 512 + z * 64 + 64]
            out[2 * z + r, 64:, :] = tail


def assemble_kernel(pos, *refs):
    *parts, cross, gate, bias = refs
    x, y = pos[0], pos[1]

    def place(from_x, from_y, first, value):
        start = pl.multiple_of((from_x & 1) * 512 + from_y * 128, 128)
        rows = pl.ds(first, 256)

        @pl.when(from_x < 2)
        def _():
            cross[rows, pl.ds(start, 128)] = value

        @pl.when(from_x >= 2)
        def _():
            gate[rows, pl.ds(start, 128)] = value

    for k in range(4):
        upper, lower = parts[k], parts[4 + k]

        @pl.loop(0, 4)
        def _(m):
            first = pl.multiple_of(m * 256, 256)
            place((x - k + 4) & 3, (y - m + 4) & 3, 0, upper[pl.ds(first, 256), :])
            first = pl.multiple_of(m * (256 + TAIL), 16)
            from_x, from_y = (x - m + 4) & 3, (y - k + 4) & 3
            place(from_x, from_y, 256, lower[pl.ds(first, 256), :])
            tail = lower[pl.ds(first + 256, TAIL), :].astype(F32)
            bias[pl.ds(from_x * 4 + from_y, 1), :] = tail[0:1] + tail[1:2]


def body(
    features,
    cotangent,
    routes,
    route_weights,
    counts,
    cross_weight,
    gate_weight,
    cross_bias,
    gate_bias,
    expert_in,
    expert_out,
):
    row_count, width = features.shape
    smem = pl.BlockSpec(memory_space=pltpu.SMEM)
    vmem = pl.BlockSpec(memory_space=pltpu.VMEM)
    experts_n = NX * NZ * NY
    slots = experts_n * CAP
    rep = lax.axis_index("rep")
    at_x, at_y = lax.axis_index("x"), lax.axis_index("y")
    pos = jnp.stack([at_x, at_y]).astype(jnp.int32)
    feature_f = features.astype(F32)

    in_own, out_own = expert_in[0], expert_out[0]
    w_pieces = jnp.stack([cross_weight, gate_weight])
    w_pieces = jnp.broadcast_to(w_pieces[None], (NZ,) + w_pieces.shape).reshape(2 * NZ, 4, width)
    w_column = exchange(w_pieces, COLUMN).reshape(8 * NZ, width)
    in_other, out_other = swap(in_own), swap(out_own)
    both = jnp.concatenate([features, swap(features)], axis=0)
    j = jnp.arange(width, dtype=jnp.int32)
    major, minor, z, i = j % 512 // 128, j // 32 % 4, j // 512 * 4 + j // 8 % 4, j % 8
    kx, ky = jnp.where(j < 512, major, minor), jnp.where(j < 512, minor, major)
    natural = ((at_x - kx) % 4) * 256 + z * 32 + ((at_y - ky) % 4) * 8 + i
    order = (j[:, None] == natural[None, :]).astype(BF16)
    both = dot(both, order).astype(BF16)
    w_parts = gather_plane(w_column, 4 * NZ)
    f_parts = gather_plane(features, row_count // 2)

    flat = routes.reshape(-1)
    onehot = (flat[:, None] == jnp.arange(experts_n, dtype=jnp.int32)[None, :]).astype(BF16)
    pairs = 2 * row_count
    ids = jnp.arange(pairs, dtype=jnp.int32)
    earlier = (ids[None, :] < ids[:, None]).astype(BF16)
    position = jnp.sum(dot(earlier, onehot) * onehot.astype(F32), axis=1).astype(jnp.int32)
    slot_index = flat * CAP + position
    slot_ids = jnp.arange(slots, dtype=jnp.int32)
    slot_match = (slot_index[None, :] == slot_ids[:, None]).astype(BF16)
    by_row = slot_index.reshape(row_count, 2)
    match0 = (by_row[:, 0:1] == slot_ids[None, :]).astype(BF16)
    match1 = (by_row[:, 1:2] == slot_ids[None, :]).astype(BF16)
    match = match0 + match1

    upstream = 0.05 * counts.astype(F32)[:, None] * cotangent.astype(F32)
    out_grad = (
        (route_weights[:, :, None] * upstream[:, None, :]).astype(BF16).reshape(pairs, width)
    )
    grad_send = dot(slot_match, out_grad).astype(BF16)
    slot_grads = dispatch(grad_send, experts_n)

    acc_own, acc_sent = pl.pallas_call(
        project_kernel,
        out_shape=(jax.ShapeDtypeStruct((row_count, width), F32),) * 2,
        in_specs=[vmem] * 9,
        out_specs=(vmem, vmem),
        name="project",
    )(both, *w_parts)
    acc_got = swap(acc_sent)
    cross_term = jnp.where(rep == 0, acc_own, acc_got) + cross_bias
    gate_term = jax.nn.sigmoid(jnp.where(rep == 0, acc_got, acc_own) + gate_bias)
    crossed = (feature_f * cross_term * gate_term + feature_f).astype(BF16)
    cross_send = dot(match, crossed, ((0,), (0,))).astype(BF16)
    slot_rows = dispatch(cross_send, experts_n)

    def half(w_in, w_out):
        pre = dot(slot_rows, w_in)
        squash = jax.nn.sigmoid(pre)
        hidden = (pre * squash).astype(BF16)
        hid_grad = dot(slot_grads, w_out, ((1,), (1,)))
        pre_grad = (hid_grad * squash * (1.0 + pre * (1.0 - squash))).astype(BF16)
        return hidden, pre_grad

    hidden_own, pre_grad_own = half(in_own, out_own)
    hidden_other, pre_grad_other = half(in_other, out_other)
    back = (
        dot(pre_grad_own, in_own, ((1,), (1,)))
        + dot(pre_grad_other, in_other, ((1,), (1,)))
    ).astype(BF16)
    back_got = dispatch(back, experts_n)
    result = (dot(hidden_own, out_own) + dot(hidden_other, out_other)).astype(BF16)
    result_got = dispatch(result, experts_n)

    crossed_grad = upstream + dot(match, back_got)
    scaled = crossed_grad * feature_f * gate_term
    cross_grad = scaled.astype(BF16)
    gate_grad = (scaled * cross_term * (1.0 - gate_term)).astype(BF16)

    blocks = jnp.concatenate([cross_grad, gate_grad], axis=1)
    blocks = blocks.reshape(row_count, NX * NY, 128).transpose(1, 0, 2)
    block = exchange(blocks, PLANE)
    pieces = pl.pallas_call(
        part_kernel,
        out_shape=jax.ShapeDtypeStruct((2 * NZ, 64 + TAIL, 128), BF16),
        in_specs=[smem] + [vmem] * 9,
        out_specs=vmem,
        name="part",
    )(pos, *f_parts, block)
    arrived = exchange(pieces, COLUMN).astype(F32)
    total = jnp.sum(arrived, axis=0)
    weight_piece = total[:64].astype(BF16)
    weight_column = spread(weight_piece, "z", NZ).reshape(8 * 64, 128)
    bias_total = total[64:65] + total[65:66]
    high = bias_total.astype(BF16)
    low = (bias_total - high.astype(F32)).astype(BF16)
    column = jnp.concatenate(
        [weight_column, high, low, jnp.zeros((TAIL - 2, 128), BF16)], axis=0
    )
    g_parts = gather_plane(column, 256)
    grad_cross, grad_gate, bias = pl.pallas_call(
        assemble_kernel,
        out_shape=(
            jax.ShapeDtypeStruct((512, width), BF16),
            jax.ShapeDtypeStruct((512, width), BF16),
            jax.ShapeDtypeStruct((16, 128), F32),
        ),
        in_specs=[smem] + [vmem] * 8,
        out_specs=(vmem, vmem, vmem),
        name="assemble",
    )(pos, *g_parts)
    bias = lax.dynamic_index_in_dim(bias.reshape(2, 2, 512), rep, axis=1, keepdims=False)

    grad_in_sent = dot(slot_rows, pre_grad_other, ((0,), (0,))).astype(BF16)
    grad_out_sent = dot(hidden_other, slot_grads, ((0,), (0,))).astype(BF16)
    grad_in_got, grad_out_got = swap(grad_in_sent), swap(grad_out_sent)
    grad_in = dot(slot_rows, pre_grad_own, ((0,), (0,))) + grad_in_got.astype(F32)
    grad_out = dot(hidden_own, slot_grads, ((0,), (0,))) + grad_out_got.astype(F32)

    layer_output = (
        crossed.astype(F32)
        + route_weights[:, 0:1] * dot(match0, result_got)
        + route_weights[:, 1:2] * dot(match1, result_got)
    ).astype(BF16)
    return (
        layer_output,
        grad_cross,
        grad_gate,
        bias[0],
        bias[1],
        grad_in.astype(BF16)[None],
        grad_out.astype(BF16)[None],
    )


def solution(mesh):
    grid = Mesh(mesh.devices.reshape(NX, NZ, NY, 2), ALL)
    return jax.shard_map(
        body,
        mesh=grid,
        in_specs=(
            P(ALL, None),
            P(ALL, None),
            P(ALL, None),
            P(ALL, None),
            P(ALL),
            P(ALL, None),
            P(ALL, None),
            P(),
            P(),
            P(DP, None, "rep"),
            P(DP, "rep", None),
        ),
        out_specs=(
            P(ALL, None),
            P("rep", None),
            P("rep", None),
            P("rep"),
            P("rep"),
            P(DP, None, "rep"),
            P(DP, "rep", None),
        ),
        check_vma=False,
    )
```

```python
import jax
import jax.numpy as jnp
from jax import lax
from jax.experimental import pallas as pl
from jax.experimental.pallas import tpu as pltpu
from jax.sharding import Mesh, PartitionSpec as P


NX, NZ, NY = 4, 8, 4
ALL = ("x", "z", "y", "rep")
DP = ("x", "z", "y")
PLANE = ("x", "y")
COLUMN = ("z", "rep")
CAP = 3
TAIL = 16
F32 = jnp.float32
BF16 = jnp.bfloat16


def swap(v):
    return lax.ppermute(v, "rep", [(0, 1), (1, 0)])


def exchange(v, axes):
    return lax.all_to_all(v, axes, split_axis=0, concat_axis=0, tiled=True)


def spread(v, axes, count):
    return exchange(jnp.broadcast_to(v[None], (count,) + v.shape), axes)


def ring(v, axis):
    return [v] + [
        lax.ppermute(v, axis, [(i, (i + k) % 4) for i in range(4)]) for k in range(1, 4)
    ]


def gather_plane(v, split):
    upper = jnp.concatenate(ring(v[:split], "y"), axis=0)
    lower = jnp.concatenate(ring(v[split:], "x"), axis=0)
    return ring(upper, "x") + ring(lower, "y")


def dot(a, b, dims=((1,), (0,))):
    return lax.dot_general(a, b, (dims, ((), ())), preferred_element_type=F32)


def dispatch(rows, experts_n):
    width = rows.shape[1]
    packed = rows.reshape(experts_n, CAP * width // 128, 128)
    got = exchange(packed, DP)
    return got.reshape(experts_n * CAP, width)


def project_kernel(rows, *refs):
    *parts, own, sent = refs
    total = jnp.zeros((256, 1024), F32)
    for k, part in enumerate(parts):
        total += jnp.dot(
            rows[:, 128 * k : 128 * k + 128], part[...], preferred_element_type=F32
        )
    own[...] = total[:128]
    sent[...] = total[128:]


def part_kernel(pos, *refs):
    *parts, block, out = refs
    x, y = pos[0], pos[1]
    total = jnp.zeros((128, 1024), F32)
    bias = jnp.zeros((1, 128), F32)
    for n, part in enumerate(parts):
        sources = [((x - n + 4) & 3) * 4 + ((y - m + 4) & 3) for m in range(4)]
        got = [block[source] for source in sources]
        got = jnp.concatenate(got, axis=0)
        total += lax.dot_general(
            got, part[...], (((0,), (0,)), ((), ())), preferred_element_type=F32
        )
        bias += jnp.sum(got.astype(F32), axis=0, keepdims=True)
    part = total.T.astype(BF16)
    high = bias.astype(BF16).astype(F32)
    row = lax.broadcasted_iota(jnp.int32, (TAIL, 128), 0)
    tail = jnp.where(row == 0, high, jnp.where(row == 1, bias - high, 0.0)).astype(BF16)
    for z in range(NZ):
        for r in range(2):
            out[2 * z + r, :64, :] = part[r * 512 + z * 64 : r * 512 + z * 64 + 64]
            out[2 * z + r, 64:, :] = tail


def assemble_kernel(pos, *refs):
    *parts, cross, gate, bias = refs
    x, y = pos[0], pos[1]

    def place(from_x, from_y, first, value):
        start = pl.multiple_of((from_x & 1) * 512 + from_y * 128, 128)
        rows = pl.ds(first, 256)

        @pl.when(from_x < 2)
        def _():
            cross[rows, pl.ds(start, 128)] = value

        @pl.when(from_x >= 2)
        def _():
            gate[rows, pl.ds(start, 128)] = value

    for k in range(4):
        upper, lower = parts[k], parts[4 + k]

        @pl.loop(0, 4)
        def _(m):
            first = pl.multiple_of(m * 256, 256)
            place((x - k + 4) & 3, (y - m + 4) & 3, 0, upper[pl.ds(first, 256), :])
            first = pl.multiple_of(m * (256 + TAIL), 16)
            from_x, from_y = (x - m + 4) & 3, (y - k + 4) & 3
            place(from_x, from_y, 256, lower[pl.ds(first, 256), :])
            tail = lower[pl.ds(first + 256, TAIL), :].astype(F32)
            bias[pl.ds(from_x * 4 + from_y, 1), :] = tail[0:1] + tail[1:2]


def body(
    features,
    cotangent,
    routes,
    route_weights,
    counts,
    cross_weight,
    gate_weight,
    cross_bias,
    gate_bias,
    expert_in,
    expert_out,
):
    row_count, width = features.shape
    smem = pl.BlockSpec(memory_space=pltpu.SMEM)
    vmem = pl.BlockSpec(memory_space=pltpu.VMEM)
    experts_n = NX * NZ * NY
    slots = experts_n * CAP
    rep = lax.axis_index("rep")
    at_x, at_y = lax.axis_index("x"), lax.axis_index("y")
    pos = jnp.stack([at_x, at_y]).astype(jnp.int32)
    feature_f = features.astype(F32)

    in_own, out_own = expert_in[0], expert_out[0]
    w_pieces = jnp.stack([cross_weight, gate_weight])
    w_pieces = jnp.broadcast_to(w_pieces[None], (NZ,) + w_pieces.shape).reshape(2 * NZ, 4, width)
    w_column = exchange(w_pieces, COLUMN).reshape(8 * NZ, width)
    in_other, out_other = swap(in_own), swap(out_own)
    both = jnp.concatenate([features, swap(features)], axis=0)
    j = jnp.arange(width, dtype=jnp.int32)
    major, minor, z, i = j % 512 // 128, j // 32 % 4, j // 512 * 4 + j // 8 % 4, j % 8
    kx, ky = jnp.where(j < 512, major, minor), jnp.where(j < 512, minor, major)
    natural = ((at_x - kx) % 4) * 256 + z * 32 + ((at_y - ky) % 4) * 8 + i
    order = (j[:, None] == natural[None, :]).astype(BF16)
    both = dot(both, order).astype(BF16)
    w_parts = gather_plane(w_column, 4 * NZ)
    f_y = jnp.concatenate(ring(features, "y"), axis=0)
    f_parts = ring(f_y, "x")

    flat = routes.reshape(-1)
    onehot = (flat[:, None] == jnp.arange(experts_n, dtype=jnp.int32)[None, :]).astype(BF16)
    pairs = 2 * row_count
    ids = jnp.arange(pairs, dtype=jnp.int32)
    earlier = (ids[None, :] < ids[:, None]).astype(BF16)
    position = jnp.sum(dot(earlier, onehot) * onehot.astype(F32), axis=1).astype(jnp.int32)
    slot_index = flat * CAP + position
    slot_ids = jnp.arange(slots, dtype=jnp.int32)
    slot_match = (slot_index[None, :] == slot_ids[:, None]).astype(BF16)
    by_row = slot_index.reshape(row_count, 2)
    match0 = (by_row[:, 0:1] == slot_ids[None, :]).astype(BF16)
    match1 = (by_row[:, 1:2] == slot_ids[None, :]).astype(BF16)
    match = match0 + match1

    upstream = 0.05 * counts.astype(F32)[:, None] * cotangent.astype(F32)
    out_grad = (
        (route_weights[:, :, None] * upstream[:, None, :]).astype(BF16).reshape(pairs, width)
    )
    grad_send = dot(slot_match, out_grad).astype(BF16)
    slot_grads = dispatch(grad_send, experts_n)

    acc_own, acc_sent = pl.pallas_call(
        project_kernel,
        out_shape=(jax.ShapeDtypeStruct((row_count, width), F32),) * 2,
        in_specs=[vmem] * 9,
        out_specs=(vmem, vmem),
        name="project",
    )(both, *w_parts)
    acc_got = swap(acc_sent)
    cross_term = jnp.where(rep == 0, acc_own, acc_got) + cross_bias
    gate_term = jax.nn.sigmoid(jnp.where(rep == 0, acc_got, acc_own) + gate_bias)
    crossed = (feature_f * cross_term * gate_term + feature_f).astype(BF16)
    cross_send = dot(match, crossed, ((0,), (0,))).astype(BF16)
    slot_rows = dispatch(cross_send, experts_n)

    def half(w_in, hid_grad):
        pre = dot(slot_rows, w_in)
        squash = jax.nn.sigmoid(pre)
        hidden = (pre * squash).astype(BF16)
        pre_grad = (hid_grad * squash * (1.0 + pre * (1.0 - squash))).astype(BF16)
        return hidden, pre_grad

    hid_own = dot(slot_grads, out_own, ((1,), (1,)))
    hid_other = dot(slot_grads, out_other, ((1,), (1,)))
    hid_own, hid_other = lax.optimization_barrier((hid_own, hid_other))
    hidden_own, pre_grad_own = half(in_own, hid_own)
    hidden_other, pre_grad_other = half(in_other, hid_other)
    back = (
        dot(pre_grad_own, in_own, ((1,), (1,)))
        + dot(pre_grad_other, in_other, ((1,), (1,)))
    ).astype(BF16)
    back_got = dispatch(back, experts_n)
    result = (dot(hidden_own, out_own) + dot(hidden_other, out_other)).astype(BF16)
    result_got = dispatch(result, experts_n)

    crossed_grad = upstream + dot(match, back_got)
    scaled = crossed_grad * feature_f * gate_term
    cross_grad = scaled.astype(BF16)
    gate_grad = (scaled * cross_term * (1.0 - gate_term)).astype(BF16)

    blocks = jnp.concatenate([cross_grad, gate_grad], axis=1)
    blocks = blocks.reshape(row_count, NX * NY, 128).transpose(1, 0, 2)
    block = exchange(blocks, PLANE)
    pieces = pl.pallas_call(
        part_kernel,
        out_shape=jax.ShapeDtypeStruct((2 * NZ, 64 + TAIL, 128), BF16),
        in_specs=[smem] + [vmem] * 5,
        out_specs=vmem,
        name="part",
    )(pos, *f_parts, block)
    arrived = exchange(pieces, COLUMN).astype(F32)
    total = jnp.sum(arrived, axis=0)
    weight_piece = total[:64].astype(BF16)
    weight_column = spread(weight_piece, "z", NZ).reshape(8 * 64, 128)
    bias_total = total[64:65] + total[65:66]
    high = bias_total.astype(BF16)
    low = (bias_total - high.astype(F32)).astype(BF16)
    column = jnp.concatenate(
        [weight_column, high, low, jnp.zeros((TAIL - 2, 128), BF16)], axis=0
    )
    g_parts = gather_plane(column, 256)
    grad_cross, grad_gate, bias = pl.pallas_call(
        assemble_kernel,
        out_shape=(
            jax.ShapeDtypeStruct((512, width), BF16),
            jax.ShapeDtypeStruct((512, width), BF16),
            jax.ShapeDtypeStruct((16, 128), F32),
        ),
        in_specs=[smem] + [vmem] * 8,
        out_specs=(vmem, vmem, vmem),
        name="assemble",
    )(pos, *g_parts)
    bias = lax.dynamic_index_in_dim(bias.reshape(2, 2, 512), rep, axis=1, keepdims=False)

    grad_in_sent = dot(slot_rows, pre_grad_other, ((0,), (0,))).astype(BF16)
    grad_out_sent = dot(hidden_other, slot_grads, ((0,), (0,))).astype(BF16)
    grad_in_got, grad_out_got = swap(grad_in_sent), swap(grad_out_sent)
    grad_in = dot(slot_rows, pre_grad_own, ((0,), (0,))) + grad_in_got.astype(F32)
    grad_out = dot(hidden_own, slot_grads, ((0,), (0,))) + grad_out_got.astype(F32)

    layer_output = (
        crossed.astype(F32)
        + route_weights[:, 0:1] * dot(match0, result_got)
        + route_weights[:, 1:2] * dot(match1, result_got)
    ).astype(BF16)
    return (
        layer_output,
        grad_cross,
        grad_gate,
        bias[0],
        bias[1],
        grad_in.astype(BF16)[None],
        grad_out.astype(BF16)[None],
    )


def solution(mesh):
    grid = Mesh(mesh.devices.reshape(NX, NZ, NY, 2), ALL)
    return jax.shard_map(
        body,
        mesh=grid,
        in_specs=(
            P(ALL, None),
            P(ALL, None),
            P(ALL, None),
            P(ALL, None),
            P(ALL),
            P(ALL, None),
            P(ALL, None),
            P(),
            P(),
            P(DP, None, "rep"),
            P(DP, "rep", None),
        ),
        out_specs=(
            P(ALL, None),
            P("rep", None),
            P("rep", None),
            P("rep"),
            P("rep"),
            P(DP, None, "rep"),
            P(DP, "rep", None),
        ),
        check_vma=False,
    )
```

```python
import jax
import jax.numpy as jnp
from jax import lax
from jax.experimental import pallas as pl
from jax.experimental.pallas import tpu as pltpu
from jax.sharding import Mesh, PartitionSpec as P


NX, NZ, NY = 4, 8, 4
ALL = ("x", "z", "y", "rep")
DP = ("x", "z", "y")
PLANE = ("x", "y")
COLUMN = ("z", "rep")
CAP = 3
TAIL = 16
F32 = jnp.float32
BF16 = jnp.bfloat16


def swap(v):
    return lax.ppermute(v, "rep", [(0, 1), (1, 0)])


def exchange(v, axes):
    return lax.all_to_all(v, axes, split_axis=0, concat_axis=0, tiled=True)


def spread(v, axes, count):
    return exchange(jnp.broadcast_to(v[None], (count,) + v.shape), axes)


def ring(v, axis):
    return [v] + [
        lax.ppermute(v, axis, [(i, (i + k) % 4) for i in range(4)]) for k in range(1, 4)
    ]


def gather_plane(v, split):
    upper = jnp.concatenate(ring(v[:split], "y"), axis=0)
    lower = jnp.concatenate(ring(v[split:], "x"), axis=0)
    return ring(upper, "x") + ring(lower, "y")


def dot(a, b, dims=((1,), (0,))):
    return lax.dot_general(a, b, (dims, ((), ())), preferred_element_type=F32)


def dispatch(rows, experts_n):
    width = rows.shape[1]
    packed = rows.reshape(experts_n, CAP * width // 128, 128)
    got = exchange(packed, DP)
    return got.reshape(experts_n * CAP, width)


def mm(a, b, contract_a, contract_b):
    return lax.dot_general(
        a, b, (((contract_a,), (contract_b,)), ((), ())), preferred_element_type=F32
    )


def chunk(c):
    return pl.ds(pl.multiple_of(c * 256, 256), 256)


def project_kernel(rows, *refs):
    *parts, own, sent = refs

    @pl.loop(0, 4)
    def _(c):
        at = chunk(c)
        for half, out in ((slice(0, 128), own), (slice(128, 256), sent)):
            total = jnp.zeros((128, 256), F32)
            for k, part in enumerate(parts):
                total += mm(rows[half, 128 * k : 128 * k + 128], part[:, at], 1, 0)
            out[:, at] = total


def part_kernel(pos, *refs):
    *parts, block, out = refs
    x, y = pos[0], pos[1]
    bias = jnp.zeros((1, 128), F32)
    for source in range(16):
        bias += jnp.sum(block[source].astype(F32), axis=0, keepdims=True)
    high = bias.astype(BF16).astype(F32)
    row = lax.broadcasted_iota(jnp.int32, (TAIL, 128), 0)
    tail = jnp.where(row == 0, high, jnp.where(row == 1, bias - high, 0.0)).astype(BF16)

    @pl.loop(0, 4)
    def _(c):
        at = chunk(c)
        total = jnp.zeros((128, 256), F32)
        for n, part in enumerate(parts):
            sources = [((x - n + 4) & 3) * 4 + ((y - m + 4) & 3) for m in range(4)]
            got = jnp.concatenate([block[source] for source in sources], axis=0)
            total += mm(got, part[:, at], 0, 0)
        piece = total.T.astype(BF16)
        for q in range(4):
            target = 2 * ((c & 1) * 4 + q) + (c >> 1)
            out[target, :64, :] = piece[64 * q : 64 * q + 64]
            out[target, 64:, :] = tail


def assemble_kernel(pos, *refs):
    *parts, cross, gate, bias, sums = refs
    x, y, rep = pos[0], pos[1], pos[2]

    def place(from_x, from_y, first, value):
        start = pl.multiple_of((from_x & 1) * 512 + from_y * 128, 128)
        rows = pl.ds(first, 256)

        @pl.when(from_x < 2)
        def _():
            cross[rows, pl.ds(start, 128)] = value

        @pl.when(from_x >= 2)
        def _():
            gate[rows, pl.ds(start, 128)] = value

    for k in range(4):
        upper, lower = parts[k], parts[4 + k]

        @pl.loop(0, 4)
        def _(m):
            first = pl.multiple_of(m * 256, 256)
            place((x - k + 4) & 3, (y - m + 4) & 3, 0, upper[pl.ds(first, 256), :])
            first = pl.multiple_of(m * (256 + TAIL), 16)
            from_x, from_y = (x - m + 4) & 3, (y - k + 4) & 3
            place(from_x, from_y, 256, lower[pl.ds(first, 256), :])
            tail = lower[pl.ds(first + 256, TAIL), :].astype(F32)
            sums[pl.ds(from_x * 4 + from_y, 1), :] = tail[0:1] + tail[1:2]

    for m in range(2):
        for q in range(4):
            bias[m * 4 + q : m * 4 + q + 1, :] = sums[pl.ds(m * 8 + rep * 4 + q, 1), :]


def body(
    features,
    cotangent,
    routes,
    route_weights,
    counts,
    cross_weight,
    gate_weight,
    cross_bias,
    gate_bias,
    expert_in,
    expert_out,
):
    row_count, width = features.shape
    smem = pl.BlockSpec(memory_space=pltpu.SMEM)
    vmem = pl.BlockSpec(memory_space=pltpu.VMEM)
    experts_n = NX * NZ * NY
    slots = experts_n * CAP
    rep = lax.axis_index("rep")
    at_x, at_y = lax.axis_index("x"), lax.axis_index("y")
    pos = jnp.stack([at_x, at_y, rep]).astype(jnp.int32)
    feature_f = features.astype(F32)

    in_own, out_own = expert_in[0], expert_out[0]
    w_pieces = jnp.stack([cross_weight, gate_weight])
    w_pieces = jnp.broadcast_to(w_pieces[None], (NZ,) + w_pieces.shape).reshape(2 * NZ, 4, width)
    w_column = exchange(w_pieces, COLUMN).reshape(8 * NZ, width)
    in_other, out_other = swap(in_own), swap(out_own)
    both = jnp.concatenate([features, swap(features)], axis=0)
    j = jnp.arange(width, dtype=jnp.int32)
    major, minor, z, i = j % 512 // 128, j // 32 % 4, j // 512 * 4 + j // 8 % 4, j % 8
    kx, ky = jnp.where(j < 512, major, minor), jnp.where(j < 512, minor, major)
    natural = ((at_x - kx) % 4) * 256 + z * 32 + ((at_y - ky) % 4) * 8 + i
    order = (j[:, None] == natural[None, :]).astype(BF16)
    both = dot(both, order).astype(BF16)
    w_parts = gather_plane(w_column, 4 * NZ)
    f_y = jnp.concatenate(ring(features, "y"), axis=0)
    f_parts = ring(f_y, "x")

    flat = routes.reshape(-1)
    onehot = (flat[:, None] == jnp.arange(experts_n, dtype=jnp.int32)[None, :]).astype(BF16)
    pairs = 2 * row_count
    ids = jnp.arange(pairs, dtype=jnp.int32)
    earlier = (ids[None, :] < ids[:, None]).astype(BF16)
    position = jnp.sum(dot(earlier, onehot) * onehot.astype(F32), axis=1).astype(jnp.int32)
    slot_index = flat * CAP + position
    slot_ids = jnp.arange(slots, dtype=jnp.int32)
    slot_match = (slot_index[None, :] == slot_ids[:, None]).astype(BF16)
    by_row = slot_index.reshape(row_count, 2)
    match0 = (by_row[:, 0:1] == slot_ids[None, :]).astype(BF16)
    match1 = (by_row[:, 1:2] == slot_ids[None, :]).astype(BF16)
    match = match0 + match1

    upstream = 0.05 * counts.astype(F32)[:, None] * cotangent.astype(F32)
    out_grad = (
        (route_weights[:, :, None] * upstream[:, None, :]).astype(BF16).reshape(pairs, width)
    )
    grad_send = dot(slot_match, out_grad).astype(BF16)
    slot_grads = dispatch(grad_send, experts_n)

    acc_own, acc_sent = pl.pallas_call(
        project_kernel,
        out_shape=(jax.ShapeDtypeStruct((row_count, width), F32),) * 2,
        in_specs=[vmem] * 9,
        out_specs=(vmem, vmem),
        name="project",
    )(both, *w_parts)
    acc_got = swap(acc_sent)
    cross_term = jnp.where(rep == 0, acc_own, acc_got) + cross_bias
    gate_term = jax.nn.sigmoid(jnp.where(rep == 0, acc_got, acc_own) + gate_bias)
    crossed = (feature_f * cross_term * gate_term + feature_f).astype(BF16)
    cross_send = dot(match, crossed, ((0,), (0,))).astype(BF16)
    slot_rows = dispatch(cross_send, experts_n)

    def half(w_in, hid_grad):
        pre = dot(slot_rows, w_in)
        squash = jax.nn.sigmoid(pre)
        hidden = (pre * squash).astype(BF16)
        pre_grad = (hid_grad * squash * (1.0 + pre * (1.0 - squash))).astype(BF16)
        return hidden, pre_grad

    hid_own = dot(slot_grads, out_own, ((1,), (1,)))
    hid_other = dot(slot_grads, out_other, ((1,), (1,)))
    hid_own, hid_other = lax.optimization_barrier((hid_own, hid_other))
    hidden_own, pre_grad_own = half(in_own, hid_own)
    hidden_other, pre_grad_other = half(in_other, hid_other)
    back = (
        dot(pre_grad_own, in_own, ((1,), (1,)))
        + dot(pre_grad_other, in_other, ((1,), (1,)))
    ).astype(BF16)
    back_got = dispatch(back, experts_n)
    result = (dot(hidden_own, out_own) + dot(hidden_other, out_other)).astype(BF16)
    result_got = dispatch(result, experts_n)

    crossed_grad = upstream + dot(match, back_got)
    scaled = crossed_grad * feature_f * gate_term
    cross_grad = scaled.astype(BF16)
    gate_grad = (scaled * cross_term * (1.0 - gate_term)).astype(BF16)

    blocks = jnp.concatenate([cross_grad, gate_grad], axis=1)
    blocks = blocks.reshape(row_count, NX * NY, 128).transpose(1, 0, 2)
    block = exchange(blocks, PLANE)
    pieces = pl.pallas_call(
        part_kernel,
        out_shape=jax.ShapeDtypeStruct((2 * NZ, 64 + TAIL, 128), BF16),
        in_specs=[smem] + [vmem] * 5,
        out_specs=vmem,
        name="part",
    )(pos, *f_parts, block)
    arrived = exchange(pieces, COLUMN).astype(F32)
    total = jnp.sum(arrived, axis=0)
    weight_piece = total[:64].astype(BF16)
    weight_column = spread(weight_piece, "z", NZ).reshape(8 * 64, 128)
    bias_total = total[64:65] + total[65:66]
    high = bias_total.astype(BF16)
    low = (bias_total - high.astype(F32)).astype(BF16)
    column = jnp.concatenate(
        [weight_column, high, low, jnp.zeros((TAIL - 2, 128), BF16)], axis=0
    )
    g_parts = gather_plane(column, 256)
    grad_cross, grad_gate, bias = pl.pallas_call(
        assemble_kernel,
        out_shape=(
            jax.ShapeDtypeStruct((512, width), BF16),
            jax.ShapeDtypeStruct((512, width), BF16),
            jax.ShapeDtypeStruct((8, 128), F32),
        ),
        in_specs=[smem] + [vmem] * 8,
        out_specs=(vmem, vmem, vmem),
        scratch_shapes=[pltpu.VMEM((16, 128), F32)],
        name="assemble",
    )(pos, *g_parts)
    bias = bias.reshape(2, 512)

    grad_in_sent = dot(slot_rows, pre_grad_other, ((0,), (0,))).astype(BF16)
    grad_out_sent = dot(hidden_other, slot_grads, ((0,), (0,))).astype(BF16)
    grad_in_got, grad_out_got = swap(grad_in_sent), swap(grad_out_sent)
    grad_in = dot(slot_rows, pre_grad_own, ((0,), (0,))) + grad_in_got.astype(F32)
    grad_out = dot(hidden_own, slot_grads, ((0,), (0,))) + grad_out_got.astype(F32)

    layer_output = (
        crossed.astype(F32)
        + route_weights[:, 0:1] * dot(match0, result_got)
        + route_weights[:, 1:2] * dot(match1, result_got)
    ).astype(BF16)
    return (
        layer_output,
        grad_cross,
        grad_gate,
        bias[0],
        bias[1],
        grad_in.astype(BF16)[None],
        grad_out.astype(BF16)[None],
    )


def solution(mesh):
    grid = Mesh(mesh.devices.reshape(NX, NZ, NY, 2), ALL)
    return jax.shard_map(
        body,
        mesh=grid,
        in_specs=(
            P(ALL, None),
            P(ALL, None),
            P(ALL, None),
            P(ALL, None),
            P(ALL),
            P(ALL, None),
            P(ALL, None),
            P(),
            P(),
            P(DP, None, "rep"),
            P(DP, "rep", None),
        ),
        out_specs=(
            P(ALL, None),
            P("rep", None),
            P("rep", None),
            P("rep"),
            P("rep"),
            P(DP, None, "rep"),
            P(DP, "rep", None),
        ),
        check_vma=False,
    )
```
